256 devices in a mesh: rows: 16 (over z, core), cols: 16 (over y, x).
Axes of the slice: x: 4, y: 4, z: 8, core: 2. Of those that a mesh axis runs over, the one named last changes fastest.
Arguments:
- in_flight: bfloat16 [16, 2, 16, 128, 16, 128], P('rows', None, 'cols'), may hold values from -0.11 to 1.36
- top_boundary: bfloat16 [2, 16, 128, 16, 128], P(None, 'cols'), may hold values from -0.11 to 1.36
- peps: bfloat16 [16, 16, 4, 4, 4, 4, 2], P('rows', 'cols'), may hold values from -0.21 to 1.46
- sketch: bfloat16 [16, 2, 16, 128, 16, 128], P('rows', None, 'cols'), may hold values from -0.11 to 1.36
Outputs:
- boundary_out: float32 [16, 2, 16, 128, 16, 128], P('rows', None, 'cols')
The draws below stay inside these ranges and needn't reach their ends.
All inputs are finite; a program needn't handle non-finite values.
Results may differ from the reference program's by a relative error of at most 0.011.
Values may be sent and summed in bfloat16 or wider, within the bound.
No kernel may reach another device: no remote copies, remote signals or barrier semaphores. Data moves between devices by JAX's collectives and lax.ppermute only.
A program may use at most 128 MiB of HBM per device.

```python
import jax
import jax.numpy as jnp
from jax import lax

CHI = 128
D = 4
P_SIZE = 2
E = 16
BOUND = 2
NSEC = 16
NCOL = 16


def near_identity(key, shape, spread):
    count = len(shape)
    first = lax.broadcasted_iota(jnp.int32, shape, count - 3)
    middle = lax.broadcasted_iota(jnp.int32, shape, count - 2)
    last = lax.broadcasted_iota(jnp.int32, shape, count - 1)
    frame = jnp.where((first == last) & (middle == 0), 1.0, 0.0).astype(jnp.float32)
    noise = jax.random.uniform(key, shape, jnp.float32, -spread, spread)
    return frame + noise


def draw_in_flight(key, part):
    shape = (NSEC, BOUND, NCOL, CHI, E, CHI)
    return near_identity(jax.random.fold_in(key, 11), shape, 0.1).astype(jnp.bfloat16)


def draw_top_boundary(key, part):
    shape = (BOUND, NCOL, CHI, E, CHI)
    return near_identity(jax.random.fold_in(key, 23), shape, 0.1).astype(jnp.bfloat16)


def draw_sketch(key, part):
    shape = (NSEC, BOUND, NCOL, CHI, E, CHI)
    return near_identity(jax.random.fold_in(key, 37), shape, 0.1).astype(jnp.bfloat16)


def draw_peps(key, part):
    shape = (NSEC, NCOL, D, D, D, D, P_SIZE)
    left = lax.broadcasted_iota(jnp.int32, shape, 2)
    upper = lax.broadcasted_iota(jnp.int32, shape, 3)
    right = lax.broadcasted_iota(jnp.int32, shape, 4)
    lower = lax.broadcasted_iota(jnp.int32, shape, 5)
    phys = lax.broadcasted_iota(jnp.int32, shape, 6).astype(jnp.float32)
    empty = (left == 0) & (upper == 0) & (right == 0) & (lower == 0)
    frame = jnp.where(empty, 1.0 - 0.5 * phys, 0.0).astype(jnp.float32)
    sub = jax.random.fold_in(key, 53)
    noise = jax.random.uniform(sub, shape, jnp.float32, -0.2, 0.2)
    return (frame + noise).astype(jnp.bfloat16)


def setup_inputs(seed: int = 0) -> dict:
    seeds = jax.random.split(jax.random.key(seed), 5)
    return {
        "in_flight": draw_in_flight(jax.random.fold_in(seeds[4], 71), 0),
        "top_boundary": draw_top_boundary(jax.random.fold_in(seeds[4], 71), 0),
        "peps": draw_peps(jax.random.fold_in(seeds[4], 71), 0),
        "sketch": draw_sketch(jax.random.fold_in(seeds[4], 71), 0),
    }


def site_image(tensor_in, right_sketch, left_sketch, site_peps):
    crossed = jnp.dot(tensor_in.reshape(CHI * E, CHI).astype(jnp.float32), right_sketch.reshape(CHI, E * CHI).astype(jnp.float32), preferred_element_type=jnp.float32).astype(jnp.bfloat16).reshape(CHI, D, D, D, D, CHI)
    ket_side = jnp.einsum('auvrsb,lurdp->avsldpb', crossed.astype(jnp.float32), site_peps.astype(jnp.float32)).astype(jnp.bfloat16)
    layered = jnp.einsum('avsldpb,mvsep->almdeb', ket_side.astype(jnp.float32), site_peps.astype(jnp.float32)).astype(jnp.bfloat16)
    image = jnp.dot(left_sketch.reshape(CHI * E, CHI).T.astype(jnp.float32), layered.reshape(CHI * E, E * CHI).astype(jnp.float32), preferred_element_type=jnp.float32)
    return image.reshape(CHI, E, CHI)

def factorize(matrix):
    gram = jnp.dot(matrix.T.astype(jnp.float32), matrix.astype(jnp.float32), precision=lax.Precision.HIGHEST, preferred_element_type=jnp.float32) / (CHI * E)
    lower = jnp.linalg.cholesky(gram)
    factor = jax.scipy.linalg.solve_triangular(lower, matrix.T, lower=True).T
    carried = lower.T / jnp.sqrt(CHI * jnp.mean(lower * lower) + 1e-06)
    return (factor, carried)

def left_sweep(images):

    def advance(carried, item):
        column, image = item
        matrix = jnp.dot(carried.astype(jnp.float32), image.reshape(CHI, E * CHI).astype(jnp.float32), precision=lax.Precision.HIGHEST, preferred_element_type=jnp.float32).reshape(CHI * E, CHI)
        factor, carried_next = factorize(matrix)
        result = jnp.where(column == NCOL - 1, matrix, factor)
        return (carried_next, result.reshape(CHI, E, CHI))
    start = jnp.eye(CHI, dtype=jnp.float32)
    _, results = lax.scan(advance, start, (jnp.arange(NCOL, dtype=jnp.int32), images))
    return results

def reference(in_flight, top_boundary, peps, sketch):
    incoming = jnp.concatenate([top_boundary[None], in_flight[:-1]], axis=0)
    left_sketch = jnp.roll(sketch, 1, axis=2)

    def one_section(operands):
        bound_rows, right_rows, left_rows, section_peps = operands

        def one_boundary(inner):
            bound_row, right_row, left_row = inner
            images = lax.map(lambda item: site_image(item[0], item[1], item[2], item[3]), (bound_row, right_row, left_row, section_peps))
            return left_sweep(images)
        return lax.map(one_boundary, (bound_rows, right_rows, left_rows))
    return lax.map(one_section, (incoming, sketch, left_sketch, peps))
```

```python
import functools
import jax
import jax.numpy as jnp
from jax import lax
from jax.experimental import pallas as pl
from jax.experimental.pallas import tpu as pltpu
from jax.sharding import PartitionSpec as P

F32, BF16 = jnp.float32, jnp.bfloat16
NN = (((1,), (0,)), ((), ()))
NT = (((1,), (1,)), ((), ()))

def mm(a, b, dims=NN):
    return lax.dot_general(a, b, dims, preferred_element_type=F32)

def split(x):
    high = x.astype(BF16)
    return high, (x - high.astype(F32)).astype(BF16)

def mm3(a, b, dims=NN):
    return mm(a[0], b[0], dims) + (mm(a[0], b[1], dims) + mm(a[1], b[0], dims))

def picker(first):
    row = lax.broadcasted_iota(jnp.int32, (256, 16), 0)
    col = lax.broadcasted_iota(jnp.int32, (256, 16), 1)
    i1, i2, i3, i4 = row // 64, (row // 16) % 4, (row // 4) % 4, row % 4
    want = i1 * 4 + i3 if first else i2 * 4 + i4
    return jnp.where(want == col, 1.0, 0.0).astype(BF16)

def image_kernel(place_ref, inc_ref, top_ref, sk_ref, left_ref, site_ref, image_ref, w_ref, crossed_ref, layered_ref, acc_ref):
    one, two = picker(True), picker(False)
    joined = jnp.zeros((256, 256), F32)
    for p in range(site_ref.shape[0]):
        site = site_ref[p]
        ket = mm(mm(one, site).astype(BF16), one, NT)
        bra = mm(mm(two, site).astype(BF16), two, NT)
        joined = joined + ket * bra
    w_ref[...] = joined.astype(BF16)
    acc_ref[...] = jnp.zeros_like(acc_ref)

    def chunk(i, carry):
        rows = pl.ds(pl.multiple_of(i * 256, 256), 256)
        inc = jnp.where(place_ref[3] == 0, top_ref[rows, :], inc_ref[rows, :])
        for n in range(8):
            part = mm(inc, sk_ref[:, 256 * n:256 * n + 256]).astype(BF16)
            crossed_ref[2 * n] = part[:, :128]
            crossed_ref[2 * n + 1] = part[:, 128:]
        w = w_ref[...]
        for a in range(0, 16, 2):
            pair = jnp.concatenate([crossed_ref[:, 16 * q:16 * q + 16, :].reshape(256, 128) for q in (a, a + 1)], axis=1)
            lay = mm(w, pair).astype(BF16)
            for k, q in enumerate((a, a + 1)):
                layered_ref[:, 16 * q:16 * q + 16, :] = lay[:, 128 * k:128 * k + 128].reshape(16, 16, 128)
        left = left_ref[:, rows]
        for n in range(8):
            both = jnp.concatenate([layered_ref[2 * n], layered_ref[2 * n + 1]], axis=1)
            acc_ref[:, 256 * n:256 * n + 256] += mm(left, both)
        return carry

    lax.fori_loop(0, 8, chunk, 0)
    for e in range(16):
        flipped = acc_ref[:, 128 * e:128 * e + 128].T
        high, low = split(flipped)
        image_ref[0, 128 * e:128 * e + 128, :] = high
        image_ref[1, 128 * e:128 * e + 128, :] = low

VM = pl.BlockSpec(memory_space=pltpu.VMEM)
def image_call(place, inc, top, sk, left, site):
    return pl.pallas_call(
        image_kernel,
        out_shape=jax.ShapeDtypeStruct((2, 2048, 128), BF16),
        in_specs=[pl.BlockSpec(memory_space=pltpu.SMEM)] + [VM] * 5,
        out_specs=VM,
        scratch_shapes=[pltpu.VMEM((256, 256), BF16), pltpu.VMEM((16, 256, 128), BF16), pltpu.VMEM((16, 256, 128), BF16), pltpu.VMEM((128, 2048), F32)],
        compiler_params=pltpu.CompilerParams(vmem_limit_bytes=32 << 20),
        cost_estimate=pl.CostEstimate(flops=4 * 10**9, bytes_accessed=3 << 20, transcendentals=0),
        name="image",
    )(place, inc, top, sk, left, site)

def step(x, high, low):
    xs = split(x)
    g = jnp.zeros((128, 128), F32)
    nb = 4
    for q in range(0, 16, nb):
        rows = slice(128 * q, 128 * (q + nb))
        h, l = high[rows, :], low[rows, :]
        z = mm3((h, l), xs)
        zh, zl = split(z)
        def lanes(t):
            return jnp.concatenate([t[128 * i:128 * i + 128] for i in range(nb)], axis=1)
        zh, zl, h, l = lanes(zh), lanes(zl), lanes(h), lanes(l)
        g = g + mm3((zh, zl), (h, l), NT)
    return g * (1.0 / 2048)

def normalized(g):
    eye = lax.broadcasted_iota(jnp.int32, g.shape, 0) == lax.broadcasted_iota(jnp.int32, g.shape, 1)
    trace = jnp.sum(jnp.sum(jnp.where(eye, g, 0.0), axis=1, keepdims=True), axis=0, keepdims=True)
    return g / (trace * (1.0 / 128) + 1e-6)

def eliminate(mats, with_inverse, upper_refs, inv_refs, nb=4):
    n = 128
    tiles = [[m[8 * i:8 * i + 8, :] for i in range(n // 8)] for m in mats]
    lane = lax.broadcasted_iota(jnp.int32, (8, n), 1)
    sub = lax.broadcasted_iota(jnp.int32, (8, n), 0)
    inv = [[jnp.where(lane == sub + 8 * i, 1.0, 0.0) for i in range(n // 8)] if w else None for w in with_inverse]
    for k in range(0, n, nb):
        t = k // 8
        for m in range(len(mats)):
            tile = tiles[m][t]
            rows, cols, erows = [], [], []
            for i in range(nb):
                s = k + i - 8 * t
                rows.append(tile[s:s + 1, :])
                if with_inverse[m]:
                    erows.append(inv[m][t][s:s + 1, :])
            el = {}
            for i in range(nb):
                for j in range(i, nb):
                    el[i, j] = jnp.broadcast_to(rows[i][:, k + j:k + j + 1], (1, n))
            fac = {}; d = []
            for i in range(nb):
                v = el[i, i]
                for q in range(i):
                    v = v - fac[q, i] * fac[q, i]
                d.append(lax.rsqrt(v))
                for j in range(i + 1, nb):
                    v = el[i, j]
                    for q in range(i):
                        v = v - fac[q, i] * fac[q, j]
                    fac[i, j] = v * d[i]
            urows, eurows = [], []
            for i in range(nb):
                v = rows[i]
                for q in range(i):
                    v = v - fac[q, i] * urows[q]
                urows.append(v * d[i])
                if with_inverse[m]:
                    v = erows[i]
                    for q in range(i):
                        v = v - fac[q, i] * eurows[q]
                    eurows.append(v * d[i])
            for i in range(nb):
                keep = lax.broadcasted_iota(jnp.int32, (1, n), 1) >= k + i
                upper_refs[m][k + i:k + i + 1, :] = jnp.where(keep, urows[i], 0.0)
                if with_inverse[m]:
                    inv_refs[m][k + i:k + i + 1, :] = eurows[i]
            first = (k + nb) // 8
            for tt in range(first, n // 8):
                tl = tiles[m][tt]
                cs = []
                for i in range(nb):
                    c = jnp.broadcast_to(tl[:, k + i:k + i + 1], (8, n))
                    for q in range(i):
                        c = c - fac[q, i] * cs[q]
                    cs.append(c * d[i])
                for i in range(nb):
                    tl = tl - cs[i] * urows[i]
                tiles[m][tt] = tl
                if with_inverse[m]:
                    e = inv[m][tt]
                    for i in range(nb):
                        e = e - cs[i] * eurows[i]
                    inv[m][tt] = e


def chain_kernel(turn, place_ref, x_ref, own0, own1, a01, a02, a03, a11, a12, a13, kept_in, send_ref, kept_ref, buf, gbuf, in_sem, out_sem):
    x_place, y_place, core = place_ref[0], place_ref[1], place_ref[2]
    sources = ((own0, a01, a02, a03), (own1, a11, a12, a13))

    @pl.when((y_place == turn) & (x_place // 2 == core))
    def _():
        for m in range(2):
            @pl.when(x_place % 2 == m)
            def _():
                for o in range(4):
                    slot = (x_place + o) % 4
                    pltpu.make_async_copy(sources[m][o], buf.at[slot], in_sem.at[slot]).start()
        g = x_ref[...]
        gbuf[0] = g
        copies = [pltpu.make_async_copy(gbuf.at[0], kept_ref.at[0], out_sem.at[0])]
        copies[0].start()
        for i in range(4):
            x = identity() if turn == 0 and i == 0 else normalized(g)
            pltpu.make_async_copy(own0, buf.at[i], in_sem.at[i]).wait()
            g = step(x, buf.at[i, 0], buf.at[i, 1])
            gbuf[i + 1] = g
            copies.append(pltpu.make_async_copy(gbuf.at[i + 1], kept_ref.at[i + 1], out_sem.at[i + 1]))
            copies[-1].start()
        send_ref[...] = g
        for copy in copies:
            copy.wait()


def identity():
    row = lax.broadcasted_iota(jnp.int32, (128, 128), 0)
    return jnp.where(row == lax.broadcasted_iota(jnp.int32, (128, 128), 1), 1.0, 0.0)


def chain_call(turn, place, x, own, arrived, kept):
    any_spec = pl.BlockSpec(memory_space=pl.ANY)
    return pl.pallas_call(
        functools.partial(chain_kernel, turn),
        out_shape=[jax.ShapeDtypeStruct((128, 128), F32), jax.ShapeDtypeStruct((5, 128, 128), F32)],
        in_specs=[pl.BlockSpec(memory_space=pltpu.SMEM), VM] + [any_spec] * 9,
        out_specs=[VM, any_spec],
        scratch_shapes=[
            pltpu.VMEM((4, 2, 2048, 128), BF16), pltpu.VMEM((5, 128, 128), F32),
            pltpu.SemaphoreType.DMA((4,)), pltpu.SemaphoreType.DMA((5,)),
        ],
        input_output_aliases={10: 1},
        compiler_params=pltpu.CompilerParams(vmem_limit_bytes=24 << 20),
        name="chain",
    )(place, x, *own, *arrived[0], *arrived[1], kept)


def final_kernel(place_ref, image0, image1, kept_ref, r1, r2, r3, out_ref, upper_ref, inverse_ref, m_ref):
    x_place, y_place, core = place_ref[0], place_ref[1], place_ref[2]
    first = (x_place == 0) & (y_place == 0)
    closing = (x_place == 3) & (y_place == 3)
    left, here = [], []
    for m in range(2):
        offset = (x_place + 8 - 2 * core - m) % 4
        pair = []
        for q in range(2):
            g = kept_ref[x_place + q]
            for o, r in enumerate((r1, r2, r3)):
                g = jnp.where(offset == o + 1, r[q], g)
            pair.append(g)
        left.append(jnp.where(first, identity(), normalized(pair[0])))
        here.append(pair[1])
    eliminate(left + here, [False, False, True, True], [upper_ref.at[i] for i in range(4)], [None, None, inverse_ref.at[0], inverse_ref.at[1]])
    for m, image in enumerate((image0, image1)):
        r = split(upper_ref[m])
        inverse = split(inverse_ref[m])
        for e in range(0, 16, 2):
            rows = slice(128 * e, 128 * e + 256)
            both = mm3(r, (image[0, rows, :], image[1, rows, :]), NT)
            for k in range(2):
                matrix = both[:, 128 * k:128 * k + 128]
                factor = mm3(split(matrix), inverse, NT)
                out_ref[0, m, 0, :, e + k, :] = jnp.where(closing, matrix, factor)


def final_call(place, images, kept, returned):
    return pl.pallas_call(
        final_kernel,
        out_shape=jax.ShapeDtypeStruct((1, 2, 1, 128, 16, 128), F32),
        in_specs=[pl.BlockSpec(memory_space=pltpu.SMEM)] + [VM] * 6,
        out_specs=VM,
        scratch_shapes=[pltpu.VMEM((4, 128, 128), F32), pltpu.VMEM((2, 128, 128), F32), pltpu.VMEM((8, 128), F32)],
        compiler_params=pltpu.CompilerParams(vmem_limit_bytes=32 << 20),
        name="final",
    )(place, *images, kept, *returned)


def on_device(in_flight, top_boundary, peps, sketch):
    row, col = lax.axis_index("rows"), lax.axis_index("cols")
    rows, cols = lax.axis_size("rows"), lax.axis_size("cols")
    x_place, y_place, core = col % 4, col // 4, row % 2
    place = jnp.stack([x_place, y_place, core, row]).astype(jnp.int32)
    both = ("rows", "cols")
    site = jnp.transpose(peps[0, 0], (4, 3, 0, 2, 1)).reshape(2, 16, 16)
    down = [(i, i + 1) for i in range(rows - 1)]
    right = [(i, (i + 1) % cols) for i in range(cols)]
    own_sketch = sketch[0, :, 0]
    flipped = jnp.swapaxes(own_sketch.reshape(2, 2048, 128), 1, 2)
    images = []
    for m in range(2):
        arrived = lax.ppermute(in_flight[0, m, 0].reshape(2048, 128), "rows", down)
        left = lax.ppermute(flipped[m], "cols", right)
        images.append(image_call(place, arrived, top_boundary[m, 0].reshape(2048, 128), own_sketch[m].reshape(128, 2048), left, site))

    def group(m, offset, outward):
        pairs = []
        for r in range(rows):
            for y in range(4):
                host = 2 * (r % 2) + m
                other = (host + offset) % 4
                a, b = r * cols + 4 * y + host, r * cols + 4 * y + other
                pairs.append((a, b) if outward else (b, a))
        return pairs

    arrivals = [[lax.ppermute(images[m], both, group(m, o, False)) for o in (1, 2, 3)] for m in range(2)]
    kept = jnp.zeros((5, 128, 128), F32)
    x = jnp.zeros((128, 128), F32)
    for turn in range(4):
        sent, kept = chain_call(turn, place, x, images, arrivals, kept)
        if turn < 3:
            pairs = [(r * cols + 4 * turn + 2 * (r % 2) + m, r * cols + 4 * turn + 4 + 2 * (r % 2) + m) for r in range(rows) for m in range(2)]
            x = lax.ppermute(sent, both, pairs)
    returned = []
    for o in (1, 2, 3):
        mine = lax.dynamic_slice(kept, ((x_place + o) % 4, 0, 0), (2, 128, 128))
        returned.append(lax.ppermute(mine, both, group(0, o, True) + group(1, o, True)))
    return final_call(place, images, kept, returned)


def solution(mesh):
    return jax.shard_map(
        on_device,
        mesh=mesh,
        in_specs=(
            P("rows", None, "cols", None, None, None),
            P(None, "cols", None, None, None),
            P("rows", "cols", None, None, None, None, None),
            P("rows", None, "cols", None, None, None),
        ),
        out_specs=P("rows", None, "cols", None, None, None),
        check_vma=False,
    )
```

```python
import functools
import jax
import jax.numpy as jnp
from jax import lax
from jax.experimental import pallas as pl
from jax.experimental.pallas import tpu as pltpu
from jax.sharding import PartitionSpec as P

F32, BF16 = jnp.float32, jnp.bfloat16
NN = (((1,), (0,)), ((), ()))
NT = (((1,), (1,)), ((), ()))

def mm(a, b, dims=NN):
    return lax.dot_general(a, b, dims, preferred_element_type=F32)

def split(x):
    high = x.astype(BF16)
    return high, (x - high.astype(F32)).astype(BF16)

def mm3(a, b, dims=NN):
    return mm(a[0], b[0], dims) + (mm(a[0], b[1], dims) + mm(a[1], b[0], dims))

def picker(first):
    row = lax.broadcasted_iota(jnp.int32, (256, 16), 0)
    col = lax.broadcasted_iota(jnp.int32, (256, 16), 1)
    i1, i2, i3, i4 = row // 64, (row // 16) % 4, (row // 4) % 4, row % 4
    want = i1 * 4 + i3 if first else i2 * 4 + i4
    return jnp.where(want == col, 1.0, 0.0).astype(BF16)

ROWS = 512


def layered_kernel(place_ref, inc_ref, top_ref, sk_ref, site_ref, layered_ref, w_ref, crossed_ref):
    one, two = picker(True), picker(False)
    joined = jnp.zeros((256, 256), F32)
    for p in range(site_ref.shape[0]):
        site = site_ref[p]
        ket = mm(mm(one, site).astype(BF16), one, NT)
        bra = mm(mm(two, site).astype(BF16), two, NT)
        joined = joined + ket * bra
    w_ref[...] = joined.astype(BF16)
    for m in range(2):
        def chunk(i, carry, m=m):
            start = pl.multiple_of(i * ROWS, ROWS)
            rows = pl.ds(start, ROWS)
            inc = jnp.where(place_ref[3] == 0, top_ref[m, rows, :], inc_ref[m, rows, :])
            for n in range(8):
                part = mm(inc, sk_ref[m, :, 256 * n:256 * n + 256]).astype(BF16)
                crossed_ref[2 * n] = part[:, :128]
                crossed_ref[2 * n + 1] = part[:, 128:]
            w = w_ref[...]
            for a in range(0, ROWS // 16, 2):
                pair = jnp.concatenate([crossed_ref[:, 16 * q:16 * q + 16, :].reshape(256, 128) for q in (a, a + 1)], axis=1)
                lay = mm(w, pair).astype(BF16)
                for k in range(2):
                    layered_ref[m, :, pl.ds(start + 16 * (a + k), 16), :] = lay[:, 128 * k:128 * k + 128].reshape(16, 16, 128)
            return carry

        lax.fori_loop(0, 2048 // ROWS, chunk, 0)


def image_kernel(layered_ref, left_ref, image0_ref, image1_ref):
    for m, image_ref in enumerate((image0_ref, image1_ref)):
        left = left_ref[m].T
        for n in range(0, 16, 2):
            wide = mm(left, cat(layered_ref[m, n], layered_ref[m, n + 1], 1))
            for e in range(2):
                high, low = split(wide[:, 128 * e:128 * e + 128].T)
                rows = slice(128 * (n + e), 128 * (n + e) + 128)
                image_ref[0, rows, :] = high
                image_ref[1, rows, :] = low


VM = pl.BlockSpec(memory_space=pltpu.VMEM)
SCALARS = pl.BlockSpec(memory_space=pltpu.SMEM)


def layered_call(place, inc, top, sk, site):
    return pl.pallas_call(
        layered_kernel,
        out_shape=jax.ShapeDtypeStruct((2, 16, 2048, 128), BF16),
        in_specs=[SCALARS] + [VM] * 4,
        out_specs=VM,
        scratch_shapes=[pltpu.VMEM((256, 256), BF16), pltpu.VMEM((16, ROWS, 128), BF16)],
        compiler_params=pltpu.CompilerParams(vmem_limit_bytes=8 << 20),
        cost_estimate=pl.CostEstimate(flops=1000, bytes_accessed=1000, transcendentals=0),
        name="layered",
    )(place, inc, top, sk, site)


def image_call(layered, left):
    return pl.pallas_call(
        image_kernel,
        out_shape=[jax.ShapeDtypeStruct((2, 2048, 128), BF16)] * 2,
        in_specs=[VM] * 2,
        out_specs=[VM] * 2,
        compiler_params=pltpu.CompilerParams(vmem_limit_bytes=8 << 20),
        cost_estimate=pl.CostEstimate(flops=1000, bytes_accessed=1000, transcendentals=0),
        name="image",
    )(layered, left)


def cat(a, b, axis):
    return jnp.concatenate([a, b], axis=axis)


def lanes(t):
    return jnp.concatenate([t[128 * i:128 * i + 128] for i in range(t.shape[0] // 128)], axis=1)


def step(x, image):
    xh, xl = split(x)
    w = cat(xh, xl, 1)
    h, l = image[0], image[1]
    z = mm(cat(h, l, 1), cat(w, w, 0))
    zh, zl = split(z[:, :128] + z[:, 128:])
    g = mm(cat(lanes(zh), lanes(zl), 0), cat(lanes(h), lanes(l), 0), NT)
    return (g[:128, :128] + (g[:128, 128:] + g[128:, :128]) + g[128:, 128:]) * (1.0 / 2048)


def normalized(g):
    eye = lax.broadcasted_iota(jnp.int32, g.shape, 0) == lax.broadcasted_iota(jnp.int32, g.shape, 1)
    trace = jnp.sum(jnp.sum(jnp.where(eye, g, 0.0), axis=1, keepdims=True), axis=0, keepdims=True)
    return g / (trace * (1.0 / 128) + 1e-6)

def eliminate(mats, with_inverse, upper_refs, inv_refs, nb=4):
    n = 128
    tiles = [[m[8 * i:8 * i + 8, :] for i in range(n // 8)] for m in mats]
    lane = lax.broadcasted_iota(jnp.int32, (8, n), 1)
    sub = lax.broadcasted_iota(jnp.int32, (8, n), 0)
    inv = [[jnp.where(lane == sub + 8 * i, 1.0, 0.0) for i in range(n // 8)] if w else None for w in with_inverse]
    for k in range(0, n, nb):
        t = k // 8
        for m in range(len(mats)):
            tile = tiles[m][t]
            rows, cols, erows = [], [], []
            for i in range(nb):
                s = k + i - 8 * t
                rows.append(tile[s:s + 1, :])
                if with_inverse[m]:
                    erows.append(inv[m][t][s:s + 1, :])
            el = {}
            for i in range(nb):
                for j in range(i, nb):
                    el[i, j] = jnp.broadcast_to(rows[i][:, k + j:k + j + 1], (1, n))
            fac = {}; d = []
            for i in range(nb):
                v = el[i, i]
                for q in range(i):
                    v = v - fac[q, i] * fac[q, i]
                d.append(lax.rsqrt(v))
                for j in range(i + 1, nb):
                    v = el[i, j]
                    for q in range(i):
                        v = v - fac[q, i] * fac[q, j]
                    fac[i, j] = v * d[i]
            urows, eurows = [], []
            for i in range(nb):
                v = rows[i]
                for q in range(i):
                    v = v - fac[q, i] * urows[q]
                urows.append(v * d[i])
                if with_inverse[m]:
                    v = erows[i]
                    for q in range(i):
                        v = v - fac[q, i] * eurows[q]
                    eurows.append(v * d[i])
            for i in range(nb):
                keep = lax.broadcasted_iota(jnp.int32, (1, n), 1) >= k + i
                upper_refs[m][k + i:k + i + 1, :] = jnp.where(keep, urows[i], 0.0)
                if with_inverse[m]:
                    inv_refs[m][k + i:k + i + 1, :] = eurows[i]
            first = (k + nb) // 8
            for tt in range(first, n // 8):
                tl = tiles[m][tt]
                cs = []
                for i in range(nb):
                    c = jnp.broadcast_to(tl[:, k + i:k + i + 1], (8, n))
                    for q in range(i):
                        c = c - fac[q, i] * cs[q]
                    cs.append(c * d[i])
                for i in range(nb):
                    tl = tl - cs[i] * urows[i]
                tiles[m][tt] = tl
                if with_inverse[m]:
                    e = inv[m][tt]
                    for i in range(nb):
                        e = e - cs[i] * eurows[i]
                    inv[m][tt] = e


ANY = pl.BlockSpec(memory_space=pl.ANY)
SMALL = pl.CostEstimate(flops=1000, bytes_accessed=1000, transcendentals=0)
SQUARE = jax.ShapeDtypeStruct((128, 128), F32)
PAIR = jax.ShapeDtypeStruct((2, 128, 128), F32)
QUAD = jax.ShapeDtypeStruct((2, 2, 128, 128), F32)


def params(mib):
    return pltpu.CompilerParams(vmem_limit_bytes=mib << 20)


def identity():
    row = lax.broadcasted_iota(jnp.int32, (128, 128), 0)
    return jnp.where(row == lax.broadcasted_iota(jnp.int32, (128, 128), 1), 1.0, 0.0)


def single_kernel(turn, place_ref, x_ref, image0, image1, kept_in, *rest):
    sends, kept_ref, sem = rest[:-2], rest[-2], rest[-1]

    @pl.when((place_ref[1] == 0) & (place_ref[0] == turn))
    def _():
        copies = [pltpu.make_async_copy(x_ref, kept_ref.at[0], sem.at[0])]
        copies[0].start()
        for m, image in enumerate((image0, image1)):
            x = identity() if turn == 0 else normalized(x_ref[m])
            g = step(x, image)
            send = sends[0].at[m] if len(sends) == 1 else sends[m]
            send[...] = g
            copies.append(pltpu.make_async_copy(send, kept_ref.at[1, m], sem.at[1 + m]))
            copies[-1].start()
        for copy in copies:
            copy.wait()


def single_call(turn, place, x, images, kept):
    sends = [SQUARE, SQUARE] if turn == 3 else [PAIR]
    return pl.pallas_call(
        functools.partial(single_kernel, turn),
        out_shape=sends + [QUAD],
        in_specs=[SCALARS, VM, VM, VM, ANY],
        out_specs=[VM] * len(sends) + [ANY],
        scratch_shapes=[pltpu.SemaphoreType.DMA((3,))],
        input_output_aliases={4: len(sends)},
        compiler_params=params(16),
        cost_estimate=SMALL,
        name="single",
    )(place, x, *images, kept)


def collect_kernel(place_ref, own0, own1, a01, a02, a03, a11, a12, a13, out_ref, sem):
    x_place, y_place, core = place_ref[0], place_ref[1], place_ref[2]
    sources = ((own0, a01, a02, a03), (own1, a11, a12, a13))

    @pl.when((y_place > 0) & (x_place // 2 == core))
    def _():
        for m in range(2):
            @pl.when(x_place % 2 == m)
            def _():
                for o in range(4):
                    pltpu.make_async_copy(sources[m][o], out_ref.at[(x_place + o) % 4], sem.at[o]).start()
        for o in range(4):
            pltpu.make_async_copy(own0, out_ref.at[o], sem.at[o]).wait()


def collect_call(place, images, arrived):
    return pl.pallas_call(
        collect_kernel,
        out_shape=jax.ShapeDtypeStruct((4, 2, 2048, 128), BF16),
        in_specs=[SCALARS] + [ANY] * 8,
        out_specs=ANY,
        scratch_shapes=[pltpu.SemaphoreType.DMA((4,))],
        compiler_params=params(4),
        cost_estimate=SMALL,
        name="collect",
    )(place, *images, *arrived[0], *arrived[1])


def chain_kernel(turn, place_ref, xa_ref, xb_ref, images, i0, i1, i2, i3, send_ref, r0, r1, r2, r3, gbuf, sem):
    x_place, y_place, core = place_ref[0], place_ref[1], place_ref[2]

    @pl.when((y_place == turn) & (x_place // 2 == core))
    def _():
        g = jnp.where(x_place % 2 == 0, xa_ref[...], xb_ref[...])
        gbuf[0] = g
        for i in range(4):
            if turn < 3 or i < 3:
                g = step(normalized(g), images.at[i])
            gbuf[i + 1] = g
        send_ref[...] = g
        copies = [pltpu.make_async_copy(gbuf.at[pl.ds((x_place + o) % 4, 2)], r, sem.at[o]) for o, r in enumerate((r0, r1, r2, r3))]
        for copy in copies:
            copy.start()
        for copy in copies:
            copy.wait()


def chain_call(turn, place, xa, xb, images, returns):
    return pl.pallas_call(
        functools.partial(chain_kernel, turn),
        out_shape=[SQUARE] + [PAIR] * 4,
        in_specs=[SCALARS, VM, VM, VM] + [ANY] * 4,
        out_specs=[VM] + [ANY] * 4,
        scratch_shapes=[pltpu.VMEM((5, 128, 128), F32), pltpu.SemaphoreType.DMA((4,))],
        input_output_aliases={4: 1, 5: 2, 6: 3, 7: 4},
        compiler_params=params(16),
        cost_estimate=SMALL,
        name="chain",
    )(place, xa, xb, images, *returns)


def final_kernel(place_ref, image0, image1, kept_ref, r0, r1, r2, r3, out_ref, upper_ref, inverse_ref, result, sem):
    x_place, y_place, core = place_ref[0], place_ref[1], place_ref[2]
    first = (x_place == 0) & (y_place == 0)
    closing = (x_place == 3) & (y_place == 3)
    left, here = [], []
    for m in range(2):
        offset = jnp.where(y_place == 0, -1, (x_place + 8 - 2 * core - m) % 4)
        pair = []
        for q in range(2):
            g = kept_ref[q, m]
            for o, r in enumerate((r0, r1, r2, r3)):
                g = jnp.where(offset == o, r[q], g)
            pair.append(g)
        left.append(jnp.where(first, identity(), normalized(pair[0])))
        here.append(pair[1])
    eliminate(left + here, [False, False, True, True], [upper_ref.at[i] for i in range(4)], [None, None, inverse_ref.at[0], inverse_ref.at[1]])
    copies = []
    for m, image in enumerate((image0, image1)):
        rh, rl = split(upper_ref[m])
        vh, vl = split(inverse_ref[m])
        r = cat(rh, rl, 0)
        v = cat(cat(vh, vh, 1), cat(vl, vl, 1), 0)
        for q in range(4):
            rows = slice(512 * q, 512 * q + 512)
            parts = mm(r, cat(image[0, rows, :], image[1, rows, :], 0), NT)
            wide = parts[:128, :512] + (parts[:128, 512:] + parts[128:, :512])
            matrix = jnp.concatenate([wide[:, 128 * i:128 * i + 128] for i in range(4)], axis=0)
            mh, ml = split(matrix)
            f = mm(cat(mh, ml, 1), v, NT)
            f = jnp.where(closing, matrix, f[:, :128] + f[:, 128:])
            for i in range(4):
                e = 4 * q + i
                result[m, e] = f[128 * i:128 * i + 128]
                copies.append(pltpu.make_async_copy(result.at[m, e], out_ref.at[0, m, 0, :, e, :], sem))
                copies[-1].start()
    for copy in copies:
        copy.wait()


def final_call(place, images, kept, returned):
    return pl.pallas_call(
        final_kernel,
        out_shape=jax.ShapeDtypeStruct((1, 2, 1, 128, 16, 128), F32),
        in_specs=[SCALARS] + [VM] * 7,
        out_specs=ANY,
        scratch_shapes=[
            pltpu.VMEM((4, 128, 128), F32), pltpu.VMEM((2, 128, 128), F32),
            pltpu.VMEM((2, 16, 128, 128), F32), pltpu.SemaphoreType.DMA,
        ],
        compiler_params=params(16),
        cost_estimate=SMALL,
        name="final",
    )(place, *images, kept, *returned)


def on_device(in_flight, top_boundary, peps, sketch):
    row, col = lax.axis_index("rows"), lax.axis_index("cols")
    rows, cols = lax.axis_size("rows"), lax.axis_size("cols")
    place = jnp.stack([col % 4, col // 4, row % 2, row]).astype(jnp.int32)
    both = ("rows", "cols")
    site = jnp.transpose(peps[0, 0], (4, 3, 0, 2, 1)).reshape(2, 16, 16)
    down = [(i, i + 1) for i in range(rows - 1)]
    right = [(i, (i + 1) % cols) for i in range(cols)]
    top = top_boundary[:, 0].reshape(2, 2048, 128)
    arrived = lax.ppermute(in_flight.reshape(2, 2048, 128), "rows", down)
    left = lax.ppermute(sketch.reshape(2, 2048, 128), "cols", right)
    layered = layered_call(place, arrived, top, sketch.reshape(2, 128, 2048), site)
    images = image_call(layered, left)

    kept = jnp.zeros((2, 2, 128, 128), F32)
    x = jnp.zeros((2, 128, 128), F32)
    for turn in range(3):
        sent, kept = single_call(turn, place, x, images, kept)
        x = lax.ppermute(sent, both, [(r * cols + turn, r * cols + turn + 1) for r in range(rows)])
    sent0, sent1, kept = single_call(3, place, x, images, kept)
    xa, xb = (lax.ppermute(sent, both, [(r * cols + 3, r * cols + 4 + 2 * (r % 2) + m) for r in range(rows)]) for m, sent in enumerate((sent0, sent1)))

    def group(m, offset, outward):
        pairs = []
        for r in range(rows):
            for y in range(1, 4):
                host = 2 * (r % 2) + m
                other = (host + offset) % 4
                a, b = r * cols + 4 * y + host, r * cols + 4 * y + other
                pairs.append((a, b) if outward else (b, a))
        return pairs

    arrivals = [[lax.ppermute(images[m], both, group(m, o, False)) for o in (1, 2, 3)] for m in range(2)]
    gathered = collect_call(place, images, arrivals)
    returns = [jnp.zeros((2, 128, 128), F32) for _ in range(4)]
    for turn in range(1, 4):
        sent, *returns = chain_call(turn, place, xa, xb, gathered, returns)
        if turn < 3:
            pairs = [(r * cols + 4 * turn + 2 * (r % 2) + m, r * cols + 4 * turn + 4 + 2 * (r % 2) + m) for r in range(rows) for m in range(2)]
            xa = xb = lax.ppermute(sent, both, pairs)
    returned = [returns[0]] + [lax.ppermute(returns[o], both, group(0, o, True) + group(1, o, True)) for o in (1, 2, 3)]
    return final_call(place, images, kept, returned)


def solution(mesh):
    return jax.shard_map(
        on_device,
        mesh=mesh,
        in_specs=(
            P("rows", None, "cols", None, None, None),
            P(None, "cols", None, None, None),
            P("rows", "cols", None, None, None, None, None),
            P("rows", None, "cols", None, None, None),
        ),
        out_specs=P("rows", None, "cols", None, None, None),
        check_vma=False,
    )
```
